128 devices in a mesh: branch: 4 (over x_hi, core), fsdp: 32 (over y, x_lo, z).
Axes of the slice: x: 4 (x_hi: 2, x_lo: 2; x = x_hi * 2 + x_lo), y: 4, z: 4, core: 2. Of those that a mesh axis runs over, the one named last changes fastest.
Arguments:
- layer_input: bfloat16 [4, 2048, 4096], P('branch', 'fsdp'), may hold values from -6 to 6
- cotangent: bfloat16 [4, 2048, 4096], P('branch', 'fsdp'), may hold values from -0.125 to 0.125
- ffn_weights: bfloat16 [4, 3, 4096, 8192], P('branch', None, None, 'fsdp'), may hold values from -0.09375 to 0.09375
- first_moment: bfloat16 [4, 3, 4096, 8192], P('branch', None, None, 'fsdp'), may hold values from -0.29882812 to 0.29882812
- second_moment: bfloat16 [4, 3, 4096, 8192], P('branch', None, None, 'fsdp'), may hold values from 0.0049743652 to 0.049804688
- routed_rows: bfloat16 [4, 128, 4096], P('branch', 'fsdp'), may hold values from -6 to 6
- expert_ids: int32 [4, 128, 2], P('branch', 'fsdp'), may hold values from 0 to 3, all different within a row; in each aligned block of 4 rows (0 to 3, 4 to 7, ..., all dimensions but the last counted through in order) at most 3 rows name the same one
- gate_codes: int32 [4, 128, 2], P('branch', 'fsdp'), may hold values from 1 to 1024
Outputs:
- mixed_rows: bfloat16 [4, 128, 4096], P('branch', 'fsdp')
The draws below stay inside these ranges and needn't reach their ends.
Inputs may be any that keep to these rules, and one draw needn't show every extreme that they name: `expert_ids`: the two experts of a row differ. Among the 4 rows of one device (aligned blocks of rows along the second dimension) no expert is named more than 3 times, a bound that some block reaches.
All inputs are finite; a program needn't handle non-finite values.
Results may differ from the reference program's by a relative error of at most 0.008.
Values may be sent and summed in bfloat16 or wider, within the bound.
No kernel may reach another device: no remote copies, remote signals or barrier semaphores. Data moves between devices by JAX's collectives and lax.ppermute only.
A program may use at most 192 MiB of HBM per device.

```python
import math
import jax
import jax.numpy as jnp
import numpy as np
from jax import lax

D = 4096
FF = 8192
ROW_DEV = 4
BRANCHES = 4
TOKENS = 2048
ROWS = 128
CAP = 3


def with_ends(array, stream_key, low, high):
    longest = array.shape.index(max(array.shape))
    spots = []
    for shift in (0, 1):
        where = [jax.random.randint(jax.random.fold_in(stream_key, axis), (), 0, length) for axis, length in enumerate(array.shape)]
        where[longest] = (where[longest] + shift) % array.shape[longest]
        spots.append(tuple(where))
    return array.at[spots[0]].set(low).at[spots[1]].set(high)


def levels(own_key, shape, split, least, largest):
    loudness = 1.0
    for axis_at, blocks in split:
        heights = jax.random.uniform(jax.random.fold_in(jax.random.fold_in(own_key, 6), axis_at), (blocks,), jnp.float32, least / len(split), largest / len(split))
        loudness = loudness * jnp.repeat(jnp.exp(heights), shape[axis_at] // blocks).reshape((-1,) + (1,) * (len(shape) - 1 - axis_at))
    return loudness


def routed_block(rng, own, number, rows, count, top, reach, skew):
    order = jax.random.permutation(rng, count)
    heavy_load, usual = portions_of(count, rows * top, reach, skew, True), portions_of(count, rows * top, reach, skew, False)
    places = jnp.arange(count)

    def named(lengths, offset_by):
        used = int((lengths > 0).sum())
        fixed = max(1, used // 4)
        shifted = fixed + (places - fixed + offset_by * (used - fixed)) % max(1, count - fixed)
        return jnp.zeros((count,), jnp.int32).at[order[jnp.where(places < fixed, places, shifted)]].set(jnp.asarray(lengths, jnp.int32))

    lengths = jnp.where(number % 4 == 0, named(heavy_load, number // 4), named(usual, number - number // 4 - 1))
    mixed = jax.random.permutation(jax.random.fold_in(own, 3), count)
    source_of, taker = mixed[0:count // 2 * 2:2], mixed[1:count // 2 * 2:2]
    room = jnp.minimum(lengths[source_of] - 1, reach - lengths[taker]) // 2
    room = jnp.where((source_of == order[0]) | (taker == order[0]) | (lengths[taker] == 0), 0, jnp.maximum(room, 0))
    shifted = jax.random.randint(jax.random.fold_in(own, 4), (count // 2,), 0, 1 << 20) % (room + 1)
    lengths = lengths.at[source_of].add(-shifted).at[taker].add(shifted)
    members = jnp.searchsorted(jnp.cumsum(lengths), jnp.arange(rows * top), side="right").astype(jnp.int32)
    table = members.reshape(top, rows).T
    table = table[jax.random.permutation(jax.random.fold_in(own, 1), rows)]
    offset_by = jax.random.randint(jax.random.fold_in(own, 2), (rows, 1), 0, top)
    return jnp.take_along_axis(table, (jnp.arange(top)[None, :] + offset_by) % top, axis=1)


def portions_of(number_of, total, bound, slope, full):
    loads = [(1 << 20) // math.isqrt(standing ** slope) + 1 for standing in range(1, number_of + 1)]
    largest = bound if full else min(bound, max(-(-total // number_of), total * loads[0] // sum(loads)))
    least = 1 if total - largest >= number_of - 1 else 0
    given, surplus = [largest] + [least] * (number_of - 1), total - largest - least * (number_of - 1)
    while surplus > 0:
        free = [i for i in range(1, number_of) if given[i] < largest] or [i for i in range(1, number_of) if given[i] < bound]
        whole, remaining = sum([loads[i] for i in free]), surplus
        for i in free:
            extra = min(bound - given[i], max(1, remaining * loads[i] // whole), surplus)
            given[i] = given[i] + extra
            surplus = surplus - extra
    return np.array(given)


def centred(key, extent, width, most, shards=(), kind=jnp.bfloat16):
    factor_of = levels(key, extent, shards, -0.22, 0.18) if shards else 1.0
    values = jax.random.normal(key, extent, jnp.float32) * width * factor_of
    return jnp.minimum(jnp.maximum(values, -most), most).astype(kind)


def setup_inputs(seed: int = 0) -> dict:
    seeds = jax.random.split(jax.random.key(seed), 9)
    layer_input = centred(seeds[0], (BRANCHES, TOKENS, D), 1.0, 6.0, ((0, 4), (1, 32)))
    cotangent = centred(seeds[1], (BRANCHES, TOKENS, D), TOKENS ** -0.5, 0.125, ((0, 4), (1, 32)))
    ffn_weights = centred(seeds[2], (BRANCHES, 3, D, FF), D ** -0.5, 0.09375, ((0, 4), (3, 32)))
    first_moment = centred(seeds[3], (BRANCHES, 3, D, FF), 0.05, 0.29882812, ((0, 4), (3, 32)))
    second_moment = jnp.clip(jnp.exp(math.log(0.049804688) - 2.3038113 * jax.random.uniform(seeds[4], (BRANCHES, 3, D, FF), jnp.float32) ** levels(seeds[4], (BRANCHES, 3, D, FF), ((0, 4), (3, 32)), -0.2, 0.2)), 0.0049743652, 0.049804688).astype(jnp.bfloat16)
    routed_rows = centred(seeds[5], (BRANCHES, ROWS, D), 1.0, 6.0, ((0, 4), (1, 32)))
    expert_ids_keys = jax.random.split(jax.random.fold_in(seeds[6], 1), BRANCHES * ROWS // ROW_DEV)
    expert_ids_turns = jax.random.permutation(jax.random.fold_in(seeds[6], 3), BRANCHES * ROWS // ROW_DEV)
    expert_ids = jax.vmap(lambda own, number: routed_block(jax.random.fold_in(seeds[6], 2), own, number, ROW_DEV, BRANCHES, 2, CAP, 2))(expert_ids_keys, expert_ids_turns).reshape((BRANCHES, ROWS, 2))
    gate_codes = with_ends(jax.random.randint(seeds[7], (BRANCHES, ROWS, 2), 1, 1025), jax.random.fold_in(seeds[7], 1), 1, 1024).astype(jnp.int32)
    return dict(layer_input=layer_input, cotangent=cotangent, ffn_weights=ffn_weights, first_moment=first_moment, second_moment=second_moment, routed_rows=routed_rows, expert_ids=expert_ids, gate_codes=gate_codes)


beta_first = 0.9
beta_second = 0.95
step_size = 0.02
epsilon = 1e-08

def branch_update(inputs, grads_out, weights, first_moment, second_moment):
    gate_pre = jnp.dot(inputs, weights[0], preferred_element_type=jnp.float32)
    up_proj = jnp.dot(inputs, weights[1], preferred_element_type=jnp.float32)
    sigmoid_gate = jax.nn.sigmoid(gate_pre)
    active_gate = gate_pre * sigmoid_gate
    hidden = (active_gate * up_proj).astype(jnp.bfloat16)
    hidden_back = jnp.dot(grads_out, weights[2], preferred_element_type=jnp.float32)
    silu_slope = sigmoid_gate * (1.0 + gate_pre * (1.0 - sigmoid_gate))
    gate_back = (hidden_back * up_proj * silu_slope).astype(jnp.bfloat16)
    up_back = (hidden_back * active_gate).astype(jnp.bfloat16)
    grad_gate = jnp.dot(inputs.T, gate_back, preferred_element_type=jnp.float32)
    grad_up = jnp.dot(inputs.T, up_back, preferred_element_type=jnp.float32)
    grad_down = jnp.dot(grads_out.T, hidden, preferred_element_type=jnp.float32)
    gradient = jnp.stack([grad_gate, grad_up, grad_down])
    first_new = beta_first * first_moment.astype(jnp.float32) + (1.0 - beta_first) * gradient
    second_new = beta_second * second_moment.astype(jnp.float32) + (1.0 - beta_second) * gradient * gradient
    updated = weights.astype(jnp.float32) - step_size * first_new / (jnp.sqrt(second_new) + epsilon)
    return updated.astype(jnp.bfloat16)

def expert_rows(row_block, weights):
    gate_pre = jnp.dot(row_block, weights[0], preferred_element_type=jnp.float32)
    up_proj = jnp.dot(row_block, weights[1], preferred_element_type=jnp.float32)
    hidden = (gate_pre * jax.nn.sigmoid(gate_pre) * up_proj).astype(jnp.bfloat16)
    result = lax.dot_general(hidden, weights[2], (((1,), (1,)), ((), ())), preferred_element_type=jnp.float32)
    return result.astype(jnp.bfloat16)

def reference(layer_input, cotangent, ffn_weights, first_moment, second_moment, routed_rows, expert_ids, gate_codes):

    def one_branch(packed):
        return branch_update(packed[0], packed[1], packed[2], packed[3], packed[4])
    merged = lax.map(one_branch, (layer_input, cotangent, ffn_weights, first_moment, second_moment))
    every_row = routed_rows.reshape(-1, D)

    def one_expert(weights):
        return expert_rows(every_row, weights)
    outputs = lax.map(one_expert, merged).astype(jnp.float32)
    chosen = expert_ids.reshape(-1, 2)
    codes_float = gate_codes.reshape(-1, 2).astype(jnp.float32)
    shares = codes_float / lax.optimization_barrier(jnp.sum(codes_float, axis=1, keepdims=True))
    expert_range = jnp.arange(BRANCHES, dtype=jnp.int32)
    mixed = jnp.zeros(every_row.shape, jnp.float32)
    for route_slot in range(2):
        member = chosen[:, route_slot][None, :] == expert_range[:, None]
        picked = lax.optimization_barrier(jnp.sum(jnp.where(member[:, :, None], outputs, 0.0), axis=0))
        mixed = mixed + shares[:, route_slot:route_slot + 1] * picked
    return mixed.astype(jnp.bfloat16).reshape(BRANCHES, ROWS, D)
```

```python
import jax
import jax.numpy as jnp
from jax import lax
from jax.sharding import PartitionSpec as P

CAP = 3
beta_first = 0.9
beta_second = 0.95
step_size = 0.02
epsilon = 1e-08

AXES = ("branch", "fsdp")

DEVICES = [
    (xh, c, y, xl, z)
    for xh in range(2)
    for c in range(2)
    for y in range(4)
    for xl in range(2)
    for z in range(4)
]


def number(xh, c, y, xl, z):
    return ((xh % 2) * 2 + c % 2) * 32 + ((y % 4) * 2 + xl % 2) * 4 + z % 4


def pairs(target):
    return [(number(*device), number(*target(*device))) for device in DEVICES]


def stays(c, y):
    return c == y % 2


def inverse(perm):
    return [(b, a) for a, b in perm]


FAR_OR_UP = pairs(
    lambda xh, c, y, xl, z: (xh, c, y + 2, xl, z) if stays(c, y) else (xh, 1 - c, y + 1, xl, z)
)
HERE_OR_UP = pairs(
    lambda xh, c, y, xl, z: (xh, c, y, xl, z) if stays(c, y) else (xh, 1 - c, y + 1, xl, z)
)
HERE_OR_DOWN = pairs(
    lambda xh, c, y, xl, z: (xh, c, y, xl, z) if stays(c, y) else (xh, 1 - c, y - 1, xl, z)
)
Z_UP = pairs(lambda xh, c, y, xl, z: (xh, c, y, xl, z + 1))
Z_DOWN = pairs(lambda xh, c, y, xl, z: (xh, c, y, xl, z - 1))
Z_FAR = pairs(lambda xh, c, y, xl, z: (xh, c, y, xl, z + 2))
X_FLIP = pairs(lambda xh, c, y, xl, z: (xh, c, y, 1 - xl, z))
CORE = pairs(lambda xh, c, y, xl, z: (xh, 1 - c, y, xl, z))
BRANCH_FLIPS = [
    None,
    CORE,
    pairs(lambda xh, c, y, xl, z: (1 - xh, c, y, xl, z)),
    pairs(lambda xh, c, y, xl, z: (1 - xh, 1 - c, y, xl, z)),
]


def move(value, perm):
    return lax.ppermute(value, AXES, perm)


def gather_tokens(shard):
    a = move(shard, FAR_OR_UP)
    b = move(shard, HERE_OR_DOWN)
    ax = move(a, X_FLIP)
    bu, bd = move(b, Z_UP), move(b, Z_DOWN)
    au, ad = move(a, Z_UP), move(a, Z_DOWN)
    bf = move(bu, Z_UP)
    bx = move(b, X_FLIP)
    axu, axd = move(ax, Z_UP), move(ax, Z_DOWN)
    af = move(au, Z_UP)
    axf = move(axd, Z_DOWN)
    bux, bdx, bfx = move(bu, X_FLIP), move(bd, X_FLIP), move(bf, X_FLIP)
    own = [b, a, bu, bd, ax, bx, au, ad, bf, axu, axd, bux, bdx, af, axf, bfx]
    return own, [move(block, CORE) for block in own]


def swap_halves(weights):
    half = weights.shape[-1] // 2
    return move(weights[..., :half], HERE_OR_DOWN), move(weights[..., half:], HERE_OR_UP)


def gather_slots(slots):
    two = jnp.concatenate([move(slots, FAR_OR_UP), move(slots, HERE_OR_DOWN)])
    four = jnp.concatenate([two, move(two, X_FLIP)])
    own = jnp.concatenate([four, move(four, Z_UP), move(four, Z_DOWN), move(four, Z_FAR)])
    return jnp.concatenate([own, move(own, CORE)])


def reduce_slots(partial):
    wide = jnp.float32
    narrow = lambda value: value.astype(jnp.bfloat16)
    count = partial.shape[0] // 2
    own = partial[:count].astype(wide) + move(narrow(partial[count:]), CORE).astype(wide)
    step = count // 4
    four = (
        own[:step]
        + move(narrow(own[step : 2 * step]), Z_DOWN).astype(wide)
        + move(narrow(own[2 * step : 3 * step]), Z_UP).astype(wide)
        + move(narrow(own[3 * step :]), Z_FAR).astype(wide)
    )
    two = four[: step // 2] + move(narrow(four[step // 2 :]), X_FLIP).astype(wide)
    return move(narrow(two[: step // 4]), inverse(FAR_OR_UP)).astype(wide) + move(
        narrow(two[step // 4 :]), inverse(HERE_OR_DOWN)
    ).astype(wide)


def branch_update(inputs, grads_out, weights, first_moment, second_moment):
    gate_pre = jnp.dot(inputs, weights[0], preferred_element_type=jnp.float32)
    up_proj = jnp.dot(inputs, weights[1], preferred_element_type=jnp.float32)
    sigmoid_gate = jax.nn.sigmoid(gate_pre)
    active_gate = gate_pre * sigmoid_gate
    hidden = (active_gate * up_proj).astype(jnp.bfloat16)
    hidden_back = jnp.dot(grads_out, weights[2], preferred_element_type=jnp.float32)
    silu_slope = sigmoid_gate * (1.0 + gate_pre * (1.0 - sigmoid_gate))
    gate_back = (hidden_back * up_proj * silu_slope).astype(jnp.bfloat16)
    up_back = (hidden_back * active_gate).astype(jnp.bfloat16)
    grad_gate = jnp.dot(inputs.T, gate_back, preferred_element_type=jnp.float32)
    grad_up = jnp.dot(inputs.T, up_back, preferred_element_type=jnp.float32)
    grad_down = jnp.dot(grads_out.T, hidden, preferred_element_type=jnp.float32)
    gradient = jnp.stack([grad_gate, grad_up, grad_down])
    first_new = beta_first * first_moment.astype(jnp.float32) + (1.0 - beta_first) * gradient
    second_new = (
        beta_second * second_moment.astype(jnp.float32) + (1.0 - beta_second) * gradient * gradient
    )
    updated = weights.astype(jnp.float32) - step_size * first_new / (jnp.sqrt(second_new) + epsilon)
    return updated.astype(jnp.bfloat16)


def expert_hidden(slot_rows, weights):
    gate_pre = jnp.dot(slot_rows, weights[0], preferred_element_type=jnp.float32)
    up_proj = jnp.dot(slot_rows, weights[1], preferred_element_type=jnp.float32)
    return (gate_pre * jax.nn.sigmoid(gate_pre) * up_proj).astype(jnp.bfloat16)


def down_project(hidden, weights):
    return lax.dot_general(
        hidden, weights[2], (((1,), (1,)), ((), ())), preferred_element_type=jnp.float32
    )


def slot_tables(chosen, gate_codes, experts, capacity):
    row_count = chosen.shape[0]
    flat_ids = chosen.reshape(-1)
    expert_range = jnp.arange(experts, dtype=jnp.int32)
    member = (flat_ids[:, None] == expert_range[None, :]).astype(jnp.int32)
    position = jnp.sum((jnp.cumsum(member, axis=0) - 1) * member, axis=1)
    slot_index = flat_ids * capacity + position
    codes_float = gate_codes.astype(jnp.float32)
    shares = (codes_float / jnp.sum(codes_float, axis=1, keepdims=True)).reshape(-1)
    owner_row = jnp.arange(row_count * 2, dtype=jnp.int32) // 2
    slot_range = jnp.arange(experts * capacity, dtype=jnp.int32)
    select = (slot_index[:, None] == slot_range[None, :]).astype(jnp.float32)
    placing = (owner_row[:, None] == jnp.arange(row_count, dtype=jnp.int32)[None, :]).astype(
        jnp.float32
    )
    pick_rows = jnp.dot(select.T, placing, precision=lax.Precision.HIGHEST)
    combine = jnp.dot(placing.T, select * shares[:, None], precision=lax.Precision.HIGHEST)
    return (pick_rows, combine)


def exchange(rows):
    parts = [
        rows[k * CAP : (k + 1) * CAP] if flip is None else move(rows[k * CAP : (k + 1) * CAP], flip)
        for k, flip in enumerate(BRANCH_FLIPS)
    ]
    return jnp.concatenate(parts)


def per_device(
    layer_input,
    cotangent,
    ffn_weights,
    first_moment,
    second_moment,
    routed_rows,
    expert_ids,
    gate_codes,
):
    experts = lax.axis_size("branch")
    tokens = layer_input.shape[1]
    width = layer_input.shape[2]
    shard = jnp.concatenate([layer_input[0], cotangent[0]])
    own, other = gather_tokens(shard)
    w_low, w_high = swap_halves(ffn_weights[0])
    first, second, w_low, w_high = lax.optimization_barrier(
        (first_moment[0], second_moment[0], w_low, w_high)
    )
    m_low, m_high = swap_halves(first)
    v_low, v_high = swap_halves(second)

    nearby = jnp.bitwise_xor(expert_ids[0], lax.axis_index("branch"))
    pick_rows, combine = slot_tables(nearby, gate_codes[0], experts, CAP)
    dispatch = jnp.dot(
        pick_rows.astype(jnp.bfloat16), routed_rows[0], preferred_element_type=jnp.float32
    )
    slots = exchange(dispatch.astype(jnp.bfloat16))
    held = gather_slots(slots)

    blocks = own + other
    inputs_all = jnp.concatenate([block[:tokens] for block in blocks])
    grads_all = jnp.concatenate([block[tokens:] for block in blocks])
    join = lambda low, high: jnp.concatenate([low, high], axis=-1)
    merged = branch_update(
        inputs_all, grads_all, join(w_low, w_high), join(m_low, m_high), join(v_low, v_high)
    )
    partial = down_project(expert_hidden(held, merged), merged)
    expert_out = reduce_slots(partial).astype(jnp.bfloat16)
    returned = exchange(expert_out)
    mixed = jnp.dot(combine, returned.astype(jnp.float32), precision=lax.Precision.HIGHEST)
    return mixed.astype(jnp.bfloat16)[None]


def solution(mesh):
    placed = (
        P("branch", "fsdp", None),
        P("branch", "fsdp", None),
        P("branch", None, None, "fsdp"),
        P("branch", None, None, "fsdp"),
        P("branch", None, None, "fsdp"),
        P("branch", "fsdp", None),
        P("branch", "fsdp", None),
        P("branch", "fsdp", None),
    )
    return jax.shard_map(
        per_device, mesh=mesh, in_specs=placed, out_specs=P("branch", "fsdp", None), check_vma=False
    )
```

```python
import functools
import jax
import jax.numpy as jnp
from jax import lax
from jax.experimental import pallas as pl
from jax.experimental.pallas import tpu as pltpu
from jax.sharding import PartitionSpec as P

CAP = 3
beta_first = 0.9
beta_second = 0.95
step_size = 0.02
epsilon = 1e-08

AXES = ("branch", "fsdp")

DEVICES = [
    (xh, c, y, xl, z)
    for xh in range(2)
    for c in range(2)
    for y in range(4)
    for xl in range(2)
    for z in range(4)
]


def number(xh, c, y, xl, z):
    return ((xh % 2) * 2 + c % 2) * 32 + ((y % 4) * 2 + xl % 2) * 4 + z % 4


def pairs(target):
    return [(number(*device), number(*target(*device))) for device in DEVICES]


def stays(c, y):
    return c == y % 2


def staying():
    core = lax.rem(lax.axis_index("branch"), 2)
    return core == lax.rem(lax.div(lax.axis_index("fsdp"), 8), 2)


def inverse(perm):
    return [(b, a) for a, b in perm]


FAR_OR_UP = pairs(
    lambda xh, c, y, xl, z: (xh, c, y + 2, xl, z) if stays(c, y) else (xh, 1 - c, y + 1, xl, z)
)
MOVING = [device for device in DEVICES if not stays(device[1], device[2])]
UP = [
    (number(xh, c, y, xl, z), number(xh, 1 - c, y + 1, xl, z)) for xh, c, y, xl, z in MOVING
]
DOWN = [
    (number(xh, c, y, xl, z), number(xh, 1 - c, y - 1, xl, z)) for xh, c, y, xl, z in MOVING
]
Z_UP = pairs(lambda xh, c, y, xl, z: (xh, c, y, xl, z + 1))
Z_DOWN = pairs(lambda xh, c, y, xl, z: (xh, c, y, xl, z - 1))
Z_FAR = pairs(lambda xh, c, y, xl, z: (xh, c, y, xl, z + 2))
X_FLIP = pairs(lambda xh, c, y, xl, z: (xh, c, y, 1 - xl, z))
CORE = pairs(lambda xh, c, y, xl, z: (xh, 1 - c, y, xl, z))
BRANCH_FLIPS = [
    None,
    CORE,
    pairs(lambda xh, c, y, xl, z: (1 - xh, c, y, xl, z)),
    pairs(lambda xh, c, y, xl, z: (1 - xh, 1 - c, y, xl, z)),
]


def move(value, perm):
    return lax.ppermute(value, AXES, perm)


def after(values, *others):
    return lax.optimization_barrier((values, others))[0]


def halves(weights):
    half = weights.shape[-1] // 2
    return weights[..., :half], weights[..., half:]


def move_halves(parts):
    return move(parts[0], DOWN), move(parts[1], UP)


def reduce_slots(partial):
    wide = jnp.float32
    narrow = lambda value: value.astype(jnp.bfloat16)
    count = partial.shape[0] // 2
    own = partial[:count].astype(wide) + move(narrow(partial[count:]), CORE).astype(wide)
    step = count // 4
    four = (
        own[:step]
        + move(narrow(own[step : 2 * step]), Z_DOWN).astype(wide)
        + move(narrow(own[2 * step : 3 * step]), Z_UP).astype(wide)
        + move(narrow(own[3 * step :]), Z_FAR).astype(wide)
    )
    two = four[: step // 2] + move(narrow(four[step // 2 :]), X_FLIP).astype(wide)
    near = two[step // 4 :]
    return move(narrow(two[: step // 4]), inverse(FAR_OR_UP)).astype(wide) + jnp.where(
        staying(), near, move(narrow(near), inverse(DOWN)).astype(wide)
    )


def adam(weight, first_moment, second_moment, gradient):
    first_new = beta_first * first_moment.astype(jnp.float32) + (1.0 - beta_first) * gradient
    second_new = (
        beta_second * second_moment.astype(jnp.float32) + (1.0 - beta_second) * gradient * gradient
    )
    step = step_size * first_new / (jnp.sqrt(second_new) + epsilon)
    return (weight.astype(jnp.float32) - step).astype(jnp.bfloat16)


def forward_kernel(count, stay, *refs):
    blocks, (w_own, w_low, w_high) = refs[:count], refs[count : count + 3]
    x_out, g_out, gate_up, hidden = refs[count + 3 : count + 7]
    xs, gs, ws, acc, sems = refs[count + 7 :]
    tokens = blocks[0].shape[0] // 2
    half = w_low.shape[-1]
    copies = []

    def start(source, target):
        copy = pltpu.make_async_copy(source, target, sems.at[len(copies)])
        copies.append(copy)
        copy.start()
        return copy

    here = lambda i: pl.ds(i * tokens, tokens)

    def fetch_w(k):
        pending = []
        for spot, moved in ((pl.ds(0, half), w_low), (pl.ds(half, half), w_high)):
            sem = sems.at[len(copies)]
            own = pltpu.make_async_copy(w_own.at[k, :, spot], ws.at[k, :, spot], sem)
            other = pltpu.make_async_copy(moved.at[k], ws.at[k, :, spot], sem)
            pl.when(stay[0] == 1)(own.start)
            pl.when(stay[0] != 1)(other.start)
            copies.append(other)
            pending.append(other)
        return pending

    x_in = [start(blocks[i].at[pl.ds(0, tokens)], xs.at[here(i)]) for i in range(count)]
    w_gate, w_up = fetch_w(0), fetch_w(1)
    g_in = [start(blocks[i].at[pl.ds(tokens, tokens)], gs.at[here(i)]) for i in range(count)]
    w_down = fetch_w(2)
    for copy in x_in:
        copy.wait()
    stores = [start(xs, x_out)]
    depth = xs.shape[1]
    part = min(1024, depth)

    def product(index, rows):
        acc[index] = jnp.zeros_like(acc[index])

        @pl.loop(0, depth // part)
        def _(k):
            columns = pl.ds(pl.multiple_of(k * part, part), part)
            acc[index] += jnp.dot(
                rows[:, columns], ws[index, columns, :], preferred_element_type=jnp.float32
            )

    for copy in w_gate:
        copy.wait()
    product(0, xs)
    for copy in w_up:
        copy.wait()
    product(1, xs)
    for copy in g_in:
        copy.wait()
    stores.append(start(gs, g_out))
    for copy in w_down:
        copy.wait()
    product(2, gs)
    gate_pre, up_proj, hidden_back = acc[0], acc[1], acc[2]
    sigmoid_gate = jax.nn.sigmoid(gate_pre)
    active_gate = gate_pre * sigmoid_gate
    hidden[...] = (active_gate * up_proj).astype(jnp.bfloat16)
    silu_slope = sigmoid_gate * (1.0 + gate_pre * (1.0 - sigmoid_gate))
    gate_up[:, : 2 * half] = (hidden_back * up_proj * silu_slope).astype(jnp.bfloat16)
    gate_up[:, 2 * half :] = (hidden_back * active_gate).astype(jnp.bfloat16)
    for copy in stores:
        copy.wait()


def forward(blocks, stay, weights):
    count = len(blocks)
    rows, width = count * blocks[0].shape[0] // 2, blocks[0].shape[1]
    size = weights[0].shape[-1]
    place = pl.BlockSpec(memory_space=pl.ANY)
    near = pl.BlockSpec(memory_space=pltpu.VMEM)
    shape = lambda *dims: jax.ShapeDtypeStruct(dims, jnp.bfloat16)
    return pl.pallas_call(
        functools.partial(forward_kernel, count),
        out_shape=(shape(rows, width), shape(rows, width), shape(rows, 2 * size), shape(rows, size)),
        in_specs=[pl.BlockSpec(memory_space=pltpu.SMEM)] + [place] * (count + 3),
        out_specs=(place, place, near, near),
        scratch_shapes=[
            pltpu.VMEM((rows, width), jnp.bfloat16),
            pltpu.VMEM((rows, width), jnp.bfloat16),
            pltpu.VMEM((3, width, size), jnp.bfloat16),
            pltpu.VMEM((3, rows, size), jnp.float32),
            pltpu.SemaphoreType.DMA((2 * count + 8,)),
        ],
        cost_estimate=pl.CostEstimate(
            flops=6 * rows * width * size,
            bytes_accessed=8 * rows * width + 6 * width * size,
            transcendentals=rows * size,
        ),
        name="forward",
    )(stay, *blocks, *weights)


def update_kernel(count, stay, *refs):
    xs, gs = refs[:count], refs[count : 2 * count]
    gate_ups, hiddens = refs[2 * count : 3 * count], refs[3 * count : 4 * count]
    weights, firsts, seconds = (refs[4 * count + 3 * i : 4 * count + 3 * i + 3] for i in range(3))
    rows, down, slot_hidden, merged, acc = refs[4 * count + 9 :]
    size = down.shape[1]
    half = size // 2
    step = pl.program_id(0)
    first = (((0,), (0,)), ((), ()))

    def summed(lefts, rights):
        total = None
        for left, right in zip(lefts, rights):
            term = lax.dot_general(left[...], right[...], first, preferred_element_type=jnp.float32)
            total = term if total is None else total + term
        return total

    def chosen(parts, index, side):
        own = parts[0][index, :, side * half : (side + 1) * half]
        return jnp.where(stay[0] == 1, own, parts[1 + side][index])

    def updated(index, side, gradient):
        return adam(*(chosen(parts, index, side) for parts in (weights, firsts, seconds)), gradient)

    gradient = summed(xs, gate_ups)
    for index in range(2):
        for side in range(2):
            spot = (2 * index + side) * half
            merged[:, spot : spot + half] = updated(index, side, gradient[:, spot : spot + half])

    @pl.when(step == 0)
    def _():
        acc[...] = jnp.zeros_like(acc)

    acc[...] += jnp.dot(rows[...], merged[...], preferred_element_type=jnp.float32)
    gradient = summed(gs, hiddens)
    for side in range(2):
        spot = side * half
        down[:, spot : spot + half] = updated(2, side, gradient[:, spot : spot + half])

    @pl.when(step == pl.num_programs(0) - 1)
    def _():
        gate_pre, up_proj = acc[:, :size], acc[:, size:]
        slot_hidden[...] = (gate_pre * jax.nn.sigmoid(gate_pre) * up_proj).astype(jnp.bfloat16)


def update(groups, stay, weights, firsts, seconds, rows):
    count = len(groups)
    width, size = groups[0][0].shape[1], groups[0][3].shape[1]
    half = size // 2
    tile = min(256, width)
    slots = rows.shape[0]
    token_spec = lambda value: pl.BlockSpec((value.shape[0], tile), lambda j, stay: (0, j))
    whole = lambda value: pl.BlockSpec(value.shape, lambda j, stay: (0, 0))
    own = pl.BlockSpec((3, tile, size), lambda j, stay: (0, j * stay[0], 0))
    side = pl.BlockSpec((3, tile, half), lambda j, stay: (0, j * (1 - stay[0]), 0))
    xs, gs, gate_ups, hiddens = zip(*groups)
    tokens = sum(x.shape[0] for x in xs)
    return pl.pallas_call(
        functools.partial(update_kernel, count),
        out_shape=(
            jax.ShapeDtypeStruct((width, size), jnp.bfloat16),
            jax.ShapeDtypeStruct((slots, size), jnp.bfloat16),
        ),
        grid_spec=pltpu.PrefetchScalarGridSpec(
            num_scalar_prefetch=1,
            grid=(width // tile,),
            in_specs=[token_spec(v) for v in xs + gs]
            + [whole(v) for v in gate_ups + hiddens]
            + [own, side, side] * 3
            + [pl.BlockSpec((slots, tile), lambda j, stay: (0, j))],
            out_specs=(
                pl.BlockSpec((tile, size), lambda j, stay: (j, 0)),
                pl.BlockSpec((slots, size), lambda j, stay: (0, 0)),
            ),
            scratch_shapes=[
                pltpu.VMEM((tile, 2 * size), jnp.bfloat16),
                pltpu.VMEM((slots, 2 * size), jnp.float32),
            ],
        ),
        cost_estimate=pl.CostEstimate(
            flops=6 * tokens * width * size + 4 * slots * width * size,
            bytes_accessed=4 * tokens * width + 20 * width * size,
            transcendentals=3 * width * size,
        ),
        name="update",
    )(stay, *xs, *gs, *gate_ups, *hiddens, *weights, *firsts, *seconds, rows)


def down_project(hidden, weights):
    return lax.dot_general(
        hidden, weights, (((1,), (1,)), ((), ())), preferred_element_type=jnp.float32
    )


def slot_tables(chosen, gate_codes, experts, capacity):
    row_count = chosen.shape[0]
    flat_ids = chosen.reshape(-1)
    expert_range = jnp.arange(experts, dtype=jnp.int32)
    member = (flat_ids[:, None] == expert_range[None, :]).astype(jnp.int32)
    position = jnp.sum((jnp.cumsum(member, axis=0) - 1) * member, axis=1)
    slot_index = flat_ids * capacity + position
    codes_float = gate_codes.astype(jnp.float32)
    shares = (codes_float / jnp.sum(codes_float, axis=1, keepdims=True)).reshape(-1)
    owner_row = jnp.arange(row_count * 2, dtype=jnp.int32) // 2
    slot_range = jnp.arange(experts * capacity, dtype=jnp.int32)
    select = (slot_index[:, None] == slot_range[None, :]).astype(jnp.float32)
    placing = (owner_row[:, None] == jnp.arange(row_count, dtype=jnp.int32)[None, :]).astype(
        jnp.float32
    )
    pick_rows = jnp.dot(select.T, placing, precision=lax.Precision.HIGHEST)
    combine = jnp.dot(placing.T, select * shares[:, None], precision=lax.Precision.HIGHEST)
    return (pick_rows, combine)


def exchange(rows):
    parts = [
        rows[k * CAP : (k + 1) * CAP] if flip is None else move(rows[k * CAP : (k + 1) * CAP], flip)
        for k, flip in enumerate(BRANCH_FLIPS)
    ]
    return jnp.concatenate(parts)


def per_device(
    layer_input,
    cotangent,
    ffn_weights,
    first_moment,
    second_moment,
    routed_rows,
    expert_ids,
    gate_codes,
):
    experts = lax.axis_size("branch")
    width = layer_input.shape[2]
    stay = staying().astype(jnp.int32).reshape(1)
    near = lambda value, moved: jnp.where(staying(), value, moved)

    nearby = jnp.bitwise_xor(expert_ids[0], lax.axis_index("branch"))
    pick_rows, combine = slot_tables(nearby, gate_codes[0], experts, CAP)

    shard = jnp.concatenate([layer_input[0], cotangent[0]])
    a, b = move(shard, FAR_OR_UP), move(shard, DOWN)
    (a, b, picked, routed, w) = after(
        (a, b, pick_rows, routed_rows[0], halves(ffn_weights[0]))
    )
    b = near(shard, b)
    dispatch = jnp.dot(picked.astype(jnp.bfloat16), routed, preferred_element_type=jnp.float32)
    dispatch = dispatch.astype(jnp.bfloat16)
    both = lambda *blocks: list(blocks) + [move(block, CORE) for block in blocks]

    ax, bu, bd = move(a, X_FLIP), move(b, Z_UP), move(b, Z_DOWN)
    w_moved = move_halves(w)
    slots = exchange(dispatch)
    two = jnp.concatenate([move(slots, FAR_OR_UP), near(slots, move(slots, DOWN))])
    bx, au, axd = move(b, X_FLIP), move(a, Z_UP), move(ax, Z_DOWN)
    weights = (ffn_weights[0],) + w_moved
    run = lambda *blocks: forward(both(*blocks), stay, weights)

    bu_, bd_, ax_ = bu, bd, ax
    (bu_, a_, two_) = after((bu, a, two), bd, ax)
    bux, ad, bf = move(bu_, X_FLIP), move(a_, Z_DOWN), move(bu_, Z_UP)
    four = jnp.concatenate([two_, move(two_, X_FLIP)])
    groups = [run(a, b), run(ax, bu)]
    (bd_, axd_, au_, m) = after(
        (bd, axd, au, halves(first_moment[0])), bx, w_moved, groups[0][3], groups[1][3]
    )
    bdx, axf, af = move(bd_, X_FLIP), move(axd_, Z_DOWN), move(au_, Z_UP)
    m_moved = move_halves(m)
    groups += [run(bd, bx), run(au, axd)]
    (bf_, ax_, four_, v) = after(
        (bf, ax, four, halves(second_moment[0])), bux, ad, m_moved, groups[2][3], groups[3][3]
    )
    bfx, axu = move(bf_, X_FLIP), move(ax_, Z_UP)
    v_moved = move_halves(v)
    held = jnp.concatenate(
        [four_, move(four_, Z_UP), move(four_, Z_DOWN), move(four_, Z_FAR)]
    )
    held = jnp.concatenate(both(held))
    groups += [run(bux, ad), run(bf, bdx), run(axf, af), run(bfx, axu)]
    down, hidden = update(
        groups,
        stay,
        weights,
        (first_moment[0],) + m_moved,
        (second_moment[0],) + v_moved,
        held,
    )
    partial = down_project(hidden, down)
    expert_out = reduce_slots(partial).astype(jnp.bfloat16)
    returned = exchange(expert_out)
    mixed = jnp.dot(combine, returned.astype(jnp.float32), precision=lax.Precision.HIGHEST)
    return mixed.astype(jnp.bfloat16)[None]


def solution(mesh):
    placed = (
        P("branch", "fsdp", None),
        P("branch", "fsdp", None),
        P("branch", None, None, "fsdp"),
        P("branch", None, None, "fsdp"),
        P("branch", None, None, "fsdp"),
        P("branch", "fsdp", None),
        P("branch", "fsdp", None),
        P("branch", "fsdp", None),
    )
    return jax.shard_map(
        per_device, mesh=mesh, in_specs=placed, out_specs=P("branch", "fsdp", None), check_vma=False
    )
```
